32 devices in a mesh: event: 8 (over z, x), lon: 4 (over y, core).
Axes of the slice: x: 2, y: 2, z: 4, core: 2. Of those that a mesh axis runs over, the one named last changes fastest.
Arguments:
- adjoint_init: bfloat16 [8, 9, 16, 128, 128], P('event', None, None, 'lon'), may hold values from -6 to 6
- forward_state: bfloat16 [8, 8, 9, 16, 128, 128], P('event', None, None, None, 'lon'), may hold values from -3 to 3
- p_speed: float32 [16, 128, 128], P(None, 'lon'), may hold values from 0.3 to 0.5
- s_speed: float32 [16, 128, 128], P(None, 'lon'), may hold values from 0.1 to 0.2
- density: float32 [16, 128, 128], P(None, 'lon'), may hold values from 0.8 to 1.6
Outputs:
- kernels: float32 [3, 16, 128, 128], P(None, 'event', 'lon')
The draws below stay inside these ranges and needn't reach their ends.
All inputs are finite; a program needn't handle non-finite values.
Results may differ from the reference program's by a relative error of at most 0.015.
Values may be sent and summed in bfloat16 or wider, within the bound.
A program may use at most 64 MiB of HBM per device.

```python
import jax
import jax.numpy as jnp
from jax import lax

LAT = 128
LEV = 16
STEPS = 8
EVENTS = 8
NLON = 128


def raised(values, own_key, source, target, shards_of, factor):
    owner, partner = [(jnp.arange(values.shape[position]) // (values.shape[position] // shards_of)).reshape([-1 if axis == position else 1 for axis in range(values.ndim)]) for position in (source, target)]
    chosen = jax.random.permutation(own_key, shards_of)[partner]
    strong = (owner == chosen) | (owner == (partner + shards_of // 2) % shards_of)
    return jnp.where(strong, factor * values, values)


def shard_levels(stream_key, dims, shards, low, high):
    def one(axis_at, shards_of):
        heights = jax.random.uniform(jax.random.fold_in(jax.random.fold_in(stream_key, 6), axis_at), (shards_of,), jnp.float32, low / len(shards), high / len(shards))
        return jnp.repeat(jnp.exp(heights), dims[axis_at] // shards_of).reshape((-1,) + (1,) * (len(dims) - axis_at - 1))

    loudness = one(*shards[0])
    for cut in shards[1:]:
        loudness = loudness * one(*cut)
    return loudness


def centred(own_key, shape, scale, reach, pieces=(), held_as=jnp.bfloat16):
    factor_of = shard_levels(own_key, shape, pieces, -0.22, 0.18) if pieces else 1.0
    result = jax.random.normal(own_key, shape, jnp.float32) * scale * factor_of
    return jnp.minimum(jnp.maximum(result, -reach), reach).astype(held_as)


def bell_draw_with(own_key, dims, deviation, most, pieces, heavy, dtype=jnp.bfloat16):
    result = deviation * jax.random.normal(own_key, dims, jnp.float32)
    if pieces:
        result = result * shard_levels(own_key, dims, pieces, -0.22, 0.18)
    return jnp.clip(raised(result, jax.random.fold_in(own_key, 3), *heavy), -most, most).astype(dtype)


def setup_inputs(seed: int = 0) -> dict:
    key_list = jax.random.split(jax.random.key(seed), 6)
    return {
        "adjoint_init": centred(key_list[0], (EVENTS, 9, LEV, NLON, LAT), 1.0, 6.0, ((0, 8), (3, 4))),
        "forward_state": bell_draw_with(key_list[1], (EVENTS, STEPS, 9, LEV, NLON, LAT), 0.5, 3.0, ((0, 8), (4, 4)), (0, 3, 8, 2.0)),
        "p_speed": jnp.clip(0.3 + 0.19999999 * jax.random.uniform(key_list[2], (LEV, NLON, LAT), jnp.float32) ** shard_levels(key_list[2], (LEV, NLON, LAT), ((1, 4),), -0.2, 0.2), 0.3, 0.5),
        "s_speed": jnp.clip(0.1 + 0.1 * jax.random.uniform(key_list[3], (LEV, NLON, LAT), jnp.float32) ** shard_levels(key_list[3], (LEV, NLON, LAT), ((1, 4),), -0.2, 0.2), 0.1, 0.2),
        "density": jnp.clip(0.8 + 0.8 * jax.random.uniform(key_list[4], (LEV, NLON, LAT), jnp.float32) ** shard_levels(key_list[4], (LEV, NLON, LAT), ((1, 4),), -0.2, 0.2), 0.8, 1.6),
    }


def ahead_diff(values, along):
    length = values.shape[along]
    border = jnp.zeros_like(lax.slice_in_dim(values, 0, 1, axis=along))
    return jnp.concatenate([lax.slice_in_dim(values, 1, length, axis=along), border], axis=along) - values


def behind_diff(values, along):
    length = values.shape[along]
    border = jnp.zeros_like(lax.slice_in_dim(values, 0, 1, axis=along))
    return values - jnp.concatenate([border, lax.slice_in_dim(values, 0, length - 1, axis=along)], axis=along)


def cycle_ahead(values, along):
    return jnp.roll(values, -1, axis=along) - values


def cycle_behind(values, along):
    return values - jnp.roll(values, 1, axis=along)


def forcing(stress, lon_ahead, lon_behind):
    stress_xx, stress_yy, stress_zz, stress_xy, stress_xz, stress_yz = [stress[index].astype(jnp.float32) for index in range(6)]
    force_x = lon_ahead(stress_xx, 1) + behind_diff(stress_xy, 2) + behind_diff(stress_xz, 0)
    force_y = lon_behind(stress_xy, 1) + ahead_diff(stress_yy, 2) + behind_diff(stress_yz, 0)
    force_z = lon_behind(stress_xz, 1) + behind_diff(stress_yz, 2) + ahead_diff(stress_zz, 0)
    return force_x, force_y, force_z


def strain_rates(velocity, lon_ahead, lon_behind):
    speed_x, speed_y, speed_z = [velocity[index].astype(jnp.float32) for index in range(3)]
    rate_xx = lon_behind(speed_x, 1)
    rate_yy = behind_diff(speed_y, 2)
    rate_zz = behind_diff(speed_z, 0)
    rate_xy = 0.5 * (ahead_diff(speed_x, 2) + lon_ahead(speed_y, 1))
    rate_xz = 0.5 * (ahead_diff(speed_x, 0) + lon_ahead(speed_z, 1))
    rate_yz = 0.5 * (ahead_diff(speed_y, 0) + ahead_diff(speed_z, 2))
    return rate_xx, rate_yy, rate_zz, rate_xy, rate_xz, rate_yz


def update_stress(stress, strain_rate, lame_coef, shear_coef):
    rate_xx, rate_yy, rate_zz, rate_xy, rate_xz, rate_yz = strain_rate
    trace_rate = rate_xx + rate_yy + rate_zz
    twice_shear = 2.0 * shear_coef
    volume_part = lame_coef * trace_rate
    updated = [
        stress[0].astype(jnp.float32) + volume_part + twice_shear * rate_xx,
        stress[1].astype(jnp.float32) + volume_part + twice_shear * rate_yy,
        stress[2].astype(jnp.float32) + volume_part + twice_shear * rate_zz,
        stress[3].astype(jnp.float32) + twice_shear * rate_xy,
        stress[4].astype(jnp.float32) + twice_shear * rate_xz,
        stress[5].astype(jnp.float32) + twice_shear * rate_yz,
    ]
    return jnp.stack([item.astype(jnp.bfloat16) for item in updated])


def kernel_terms(velocity, strain_rate, forward_now):
    rate_xx, rate_yy, rate_zz, rate_xy, rate_xz, rate_yz = strain_rate
    forward_f = [forward_now[index].astype(jnp.float32) for index in range(9)]
    trace_rate = rate_xx + rate_yy + rate_zz
    lame_term = trace_rate * (forward_f[3] + forward_f[4] + forward_f[5])
    shear_term = 2.0 * (rate_xx * forward_f[3] + rate_yy * forward_f[4] + rate_zz * forward_f[5]
                        + 2.0 * (rate_xy * forward_f[6] + rate_xz * forward_f[7] + rate_yz * forward_f[8]))
    speed = [velocity[index].astype(jnp.float32) for index in range(3)]
    density_term = speed[0] * forward_f[0] + speed[1] * forward_f[1] + speed[2] * forward_f[2]
    return lame_term, shear_term, density_term


def combine_kernels(kernel_total, p_speed, s_speed, density):
    lame_coef = density * (p_speed * p_speed - 2.0 * s_speed * s_speed)
    shear_coef = density * s_speed * s_speed
    return jnp.stack([
        2.0 * density * p_speed * p_speed * kernel_total[0],
        2.0 * density * s_speed * s_speed * (kernel_total[1] - 2.0 * kernel_total[0]),
        density * kernel_total[2] + lame_coef * kernel_total[0] + shear_coef * kernel_total[1],
    ])


def reference(adjoint_init, forward_state, p_speed, s_speed, density):
    lame_coef = density * (p_speed * p_speed - 2.0 * s_speed * s_speed)
    shear_coef = density * s_speed * s_speed
    buoyancy = 1.0 / density

    def advance(state_pair, forward_now):
        fields, kernel_sums = state_pair
        force = forcing(fields[3:9], cycle_ahead, cycle_behind)
        velocity = jnp.stack([(fields[index].astype(jnp.float32) + buoyancy * force[index]).astype(jnp.bfloat16) for index in range(3)])
        strain_rate = strain_rates(velocity, cycle_ahead, cycle_behind)
        stress = update_stress(fields[3:9], strain_rate, lame_coef, shear_coef)
        kernel_sums = kernel_sums + jnp.stack(kernel_terms(velocity, strain_rate, forward_now))
        return (jnp.concatenate([velocity, stress]), kernel_sums), None

    def per_event(event_total, event_inputs):
        initial, forward = event_inputs
        blank_sums = jnp.zeros((3,) + p_speed.shape, jnp.float32)
        (final_fields, kernel_sums), unused = lax.scan(advance, (initial, blank_sums), forward)
        return event_total + kernel_sums, None

    kernel_total, unused = lax.scan(per_event, jnp.zeros((3,) + p_speed.shape, jnp.float32), (adjoint_init, forward_state))
    return combine_kernels(kernel_total, p_speed, s_speed, density)
```

```python
import functools

import jax
import jax.numpy as jnp
from jax import lax
from jax.experimental import pallas as pl
from jax.experimental.pallas import tpu as pltpu
from jax.sharding import PartitionSpec as P

VX, VY, VZ, XX, YY, ZZ, XY, XZ, YZ = range(9)
HALO = 4
TILE = 8
PAD = 8
UNROLL = 2


def behind_lat(a):
    lane = lax.broadcasted_iota(jnp.int32, a.shape, 1)
    return a - jnp.where(lane == 0, 0.0, pltpu.roll(a, 1, 1))


def ahead_lat(a):
    lane = lax.broadcasted_iota(jnp.int32, a.shape, 1)
    last = a.shape[1] - 1
    return jnp.where(lane == last, 0.0, pltpu.roll(a, last, 1)) - a


def kernel(
    adj_hbm, fwd_hbm, p_hbm, s_hbm, d_hbm, out_ref,
    adj, fwd, p_raw, s_raw, d_raw, w, mat, acc,
    first_out, first_in, next_out, next_in, red_out, red_in,
    local_sem, fwd_sem, halo_send, halo_recv, red_send, red_recv,
):
    levels, own, lat = p_raw.shape
    steps = fwd.shape[0]
    events, ring = lax.axis_size("event"), lax.axis_size("lon")
    me_e, me_l = lax.axis_index("event"), lax.axis_index("lon")
    right, left = lax.rem(me_l + 1, ring), lax.rem(me_l + ring - 1, ring)
    share = levels // events

    local = [
        pltpu.make_async_copy(src, dst, local_sem.at[i])
        for i, (src, dst) in enumerate(
            ((adj_hbm.at[0], adj), (d_hbm, d_raw), (p_hbm, p_raw), (s_hbm, s_raw))
        )
    ]
    for copy in local:
        copy.start()

    def fwd_copy(t):
        return pltpu.make_async_copy(fwd_hbm.at[0, t], fwd.at[t], fwd_sem.at[t])

    for t in range(steps):
        fwd_copy(t).start()

    barrier = pltpu.get_barrier_semaphore()
    for neighbour in (left, right):
        pl.semaphore_signal(
            barrier, inc=1, device_id=(me_e, neighbour), device_id_type=pl.DeviceIdType.MESH
        )
    for d in range(1, events):
        pl.semaphore_signal(
            barrier, inc=1, device_id=(lax.rem(me_e + d, events), me_l),
            device_id_type=pl.DeviceIdType.MESH,
        )

    zeros = jnp.zeros((w.shape[2], lat), jnp.float32)
    for f in (XZ, YZ, VZ):
        w[f, 0] = zeros
    for f in (ZZ, VX, VY):
        w[f, levels + 1] = zeros

    upper = lax.broadcasted_iota(jnp.int32, (TILE, lat), 0) < HALO

    def pack(get, put):
        def edges(j):
            a, b = get(j, 0), get(j + 1, 0)
            c, d = get(j, own - TILE), get(j + 1, own - TILE)
            return (
                jnp.where(upper, a, pltpu.roll(b, HALO, 0)),
                jnp.where(upper, pltpu.roll(c, HALO, 0), d),
            )

        lo, hi = edges(0), edges(2)
        for side in range(2):
            put(side, jnp.concatenate([lo[side], hi[side]], axis=0).astype(jnp.bfloat16))

    def unpack(from_right, from_left, put):
        r16, l16 = from_right.astype(jnp.float32), from_left.astype(jnp.float32)
        for half in range(2):
            r, l = (v[half * TILE:(half + 1) * TILE] for v in (r16, l16))
            put(2 * half, jnp.where(upper, r, pltpu.roll(l, HALO, 0)))
            put(2 * half + 1, jnp.where(upper, pltpu.roll(r, HALO, 0), l))

    quads = levels // 4
    local[0].wait()

    def load_fields(q, carry):
        for f in range(9):
            for j in range(4):
                rows = adj[f, q * 4 + j].astype(jnp.float32)
                w[f, q * 4 + j + 1, PAD:PAD + own, :] = rows
                if f == XX:
                    w[f, q * 4 + j + 1, PAD + own + TILE:PAD + own + 2 * TILE, :] = rows[:TILE]
        return carry

    lax.fori_loop(0, quads, load_fields, 0)

    for copy in local[1:]:
        copy.wait()

    def load_material(z, carry):
        d, p, s = d_raw[z], p_raw[z], s_raw[z]
        mat[0, z, 0:own, :] = 1.0 / d
        mat[1, z, 0:own, :] = d * (p * p - 2.0 * s * s)
        mat[2, z, 0:own, :] = d * s * s
        return carry

    lax.fori_loop(0, levels, load_material, 0)

    def pack_fields(out):
        def body(q, carry):
            for f in range(9):
                def put(side, value, f=f):
                    out[side, f, q] = value

                pack(lambda j, r, f=f: w[f, q * 4 + j + 1, PAD + r:PAD + r + TILE, :], put)
            return carry

        lax.fori_loop(0, quads, body, 0)

    def pack_material(q, carry):
        for f in range(3):
            def put(side, value, f=f):
                first_out[side, 9 + f, q] = value

            pack(lambda j, r, f=f: mat[f, q * 4 + j, r:r + TILE, :], put)
        return carry

    pack_fields(first_out)
    lax.fori_loop(0, quads, pack_material, 0)
    pl.semaphore_wait(barrier, events + 1)

    def exchange(src, dst, at):
        return [
            pltpu.make_async_remote_copy(
                src_ref=src.at[side], dst_ref=dst.at[side],
                send_sem=halo_send.at[at, side], recv_sem=halo_recv.at[at, side],
                device_id=(me_e, target), device_id_type=pl.DeviceIdType.MESH,
            )
            for side, target in ((0, left), (1, right))
        ]

    def unpack_fields(src):
        def body(q, carry):
            for f in range(9):
                def put(j, tile, f=f):
                    w[f, q * 4 + j + 1, PAD + own:PAD + own + TILE, :] = tile
                    if f in (XY, XZ):
                        w[f, q * 4 + j + 1, 0:TILE, :] = tile

                unpack(src[0, f, q], src[1, f, q], put)
            return carry

        lax.fori_loop(0, quads, body, 0)

    blocks = [(r, 2 * TILE) for r in range(0, own, 2 * TILE)] + [(own, TILE)]

    def velocity_level(z):
        for r, n in blocks:
            def ld(f, off=0, dz=0):
                return w[f, z + 1 + dz, pl.ds(PAD + r + off, n), :]

            buoy = mat[0, z, r:r + n, :]
            xy, xz, yz, zz = ld(XY), ld(XZ), ld(YZ), ld(ZZ)
            fx = (ld(XX, 1) - ld(XX)) + behind_lat(xy) + (xz - ld(XZ, 0, -1))
            fy = (xy - ld(XY, -1)) + ahead_lat(ld(YY)) + (yz - ld(YZ, 0, -1))
            fz = (xz - ld(XZ, -1)) + behind_lat(yz) + (ld(ZZ, 0, 1) - zz)
            for f, force in ((VX, fx), (VY, fy), (VZ, fz)):
                v = ld(f) + buoy * force
                w[f, z + 1, PAD + r:PAD + r + n, :] = v
                if r == 0 and f in (VY, VZ):
                    w[f, z + 1, PAD + own + TILE:PAD + own + 2 * TILE, :] = v[:TILE]
                if r == own and f == VX:
                    w[f, z + 1, 0:TILE, :] = v

    def rates(z, r, n):
        def ld(f, off=0, dz=0):
            return w[f, z + 1 + dz, pl.ds(PAD + r + off, n), :]

        vx, vy, vz = ld(VX), ld(VY), ld(VZ)
        exx = vx - ld(VX, -1)
        eyy = behind_lat(vy)
        ezz = vz - ld(VZ, 0, -1)
        gxy = ahead_lat(vx) + (ld(VY, 1) - vy)
        gxz = (ld(VX, 0, 1) - vx) + (ld(VZ, 1) - vz)
        gyz = (ld(VY, 0, 1) - vy) + ahead_lat(vz)
        return (vx, vy, vz), (exx, eyy, ezz, gxy, gxz, gyz), exx + eyy + ezz

    def terms(t, z, r, n, v, e, tr):
        F = [fwd[t, f, z, r:r + n, :].astype(jnp.float32) for f in range(9)]
        k_lame = tr * (F[3] + F[4] + F[5])
        half_shear = (e[0] * F[3] + e[1] * F[4] + e[2] * F[5]) + (
            e[3] * F[6] + e[4] * F[7] + e[5] * F[8]
        )
        k_dens = v[0] * F[0] + v[1] * F[1] + v[2] * F[2]
        return k_lame, half_shear, k_dens

    def stress_level(t, z):
        for r, n in blocks:
            v, e, tr = rates(z, r, n)
            lame, shear = mat[1, z, r:r + n, :], mat[2, z, r:r + n, :]
            volume, twice = lame * tr, shear + shear
            for i, f in enumerate((XX, YY, ZZ, XY, XZ, YZ)):
                rows = slice(PAD + r, PAD + r + n)
                s = w[f, z + 1, rows, :]
                s = (s + volume) + twice * e[i] if i < 3 else s + shear * e[i]
                w[f, z + 1, rows, :] = s
                if r == 0 and f == XX:
                    w[f, z + 1, PAD + own + TILE:PAD + own + 2 * TILE, :] = s[:TILE]
                if r == own and f in (XY, XZ):
                    w[f, z + 1, 0:TILE, :] = s
            if r < own:
                for i, term in enumerate(terms(t, z, r, n, v, e, tr)):
                    acc[i, z, r:r + n, :] += term

    def sweep(level):
        def body(i, carry):
            for j in range(UNROLL):
                level(i * UNROLL + j)
            return carry

        lax.fori_loop(0, levels // UNROLL, body, 0)

    def step(t, carry):
        sweep(velocity_level)
        fwd_copy(t).wait()
        sweep(functools.partial(stress_level, t))
        return carry

    def clear(z, carry):
        for i in range(3):
            acc[i, z] = jnp.zeros((own, lat), jnp.float32)
        return carry

    copies = exchange(first_out, first_in, 0)
    for copy in copies:
        copy.start()
    lax.fori_loop(0, levels, clear, 0)
    for copy in copies:
        copy.wait()
    unpack_fields(first_in)

    def unpack_material(q, carry):
        for f in range(3):
            def put(j, tile, f=f):
                mat[f, q * 4 + j, own:own + TILE, :] = tile

            unpack(first_in[0, 9 + f, q], first_in[1, 9 + f, q], put)
        return carry

    lax.fori_loop(0, quads, unpack_material, 0)

    for epoch in range(-(-steps // HALO)):
        if epoch:
            pack_fields(next_out.at[epoch - 1])
            copies = exchange(next_out.at[epoch - 1], next_in.at[epoch - 1], epoch)
            for copy in copies:
                copy.start()
            for copy in copies:
                copy.wait()
            unpack_fields(next_in.at[epoch - 1])
        lax.fori_loop(epoch * HALO, min((epoch + 1) * HALO, steps - 1), step, 0)

    sweep(velocity_level)
    last = steps - 1
    fwd_copy(last).wait()

    def last_levels(owner, write):
        for j in range(share):
            z = owner * share + j
            for r, n in blocks[:-1]:
                v, e, tr = rates(z, r, n)
                for i, term in enumerate(terms(last, z, r, n, v, e, tr)):
                    write(i, j, z, r, n, acc[i, z, r:r + n, :] + term)

    def red_copy(d, owner):
        return pltpu.make_async_remote_copy(
            src_ref=red_out.at[d], dst_ref=red_in.at[d],
            send_sem=red_send.at[d], recv_sem=red_recv.at[d],
            device_id=(owner, me_l), device_id_type=pl.DeviceIdType.MESH,
        )

    def send_levels(d, carry):
        owner = lax.rem(me_e + d + 1, events)

        def write(i, j, z, r, n, total):
            red_out[d, i, j, r:r + n, :] = total.astype(jnp.bfloat16)

        last_levels(owner, write)
        red_copy(d, owner).start()
        return carry

    lax.fori_loop(0, events - 1, send_levels, 0)

    def keep(i, j, z, r, n, total):
        acc[i, z, r:r + n, :] = total

    last_levels(me_e, keep)

    def finish_copies(d, carry):
        red_copy(d, lax.rem(me_e + d + 1, events)).wait()
        return carry

    lax.fori_loop(0, events - 1, finish_copies, 0)

    for j in range(share):
        z = me_e * share + j
        for r, n in blocks[:-1]:
            k_lame, half_shear, k_dens = (
                acc[i, z, r:r + n, :]
                + sum(red_in[d, i, j, r:r + n, :].astype(jnp.float32) for d in range(events - 1))
                for i in range(3)
            )
            k_shear = 2.0 * half_shear
            p, s, d = (x[z, r:r + n, :] for x in (p_raw, s_raw, d_raw))
            lame, shear = d * (p * p - 2.0 * s * s), d * s * s
            out_ref[0, j, r:r + n, :] = 2.0 * d * p * p * k_lame
            out_ref[1, j, r:r + n, :] = 2.0 * d * s * s * (k_shear - 2.0 * k_lame)
            out_ref[2, j, r:r + n, :] = d * k_dens + lame * k_lame + shear * k_shear


def shards(adjoint_init, forward_state, p_speed, s_speed, density):
    levels, own, lat = p_speed.shape
    steps = forward_state.shape[1]
    events = lax.axis_size("event")
    share, quads = levels // events, levels // 4
    epochs = -(-steps // HALO)
    f32, bf16 = jnp.float32, jnp.bfloat16
    anywhere = pl.BlockSpec(memory_space=pl.ANY)
    return pl.pallas_call(
        kernel,
        out_shape=jax.ShapeDtypeStruct((3, share, own, lat), f32),
        in_specs=[anywhere] * 5,
        out_specs=pl.BlockSpec(memory_space=pltpu.VMEM),
        scratch_shapes=[
            pltpu.VMEM(adjoint_init.shape[1:], bf16),
            pltpu.VMEM(forward_state.shape[1:], bf16),
            pltpu.VMEM(p_speed.shape, f32),
            pltpu.VMEM(p_speed.shape, f32),
            pltpu.VMEM(p_speed.shape, f32),
            pltpu.VMEM((9, levels + 2, PAD + own + 2 * TILE, lat), f32),
            pltpu.VMEM((3, levels, own + TILE, lat), f32),
            pltpu.VMEM((3, levels, own, lat), f32),
            pltpu.VMEM((2, 12, quads, 2 * TILE, lat), bf16),
            pltpu.VMEM((2, 12, quads, 2 * TILE, lat), bf16),
            pltpu.VMEM((max(epochs - 1, 1), 2, 9, quads, 2 * TILE, lat), bf16),
            pltpu.VMEM((max(epochs - 1, 1), 2, 9, quads, 2 * TILE, lat), bf16),
            pltpu.VMEM((events - 1, 3, share, own, lat), bf16),
            pltpu.VMEM((events - 1, 3, share, own, lat), bf16),
            pltpu.SemaphoreType.DMA((4,)),
            pltpu.SemaphoreType.DMA((steps,)),
            pltpu.SemaphoreType.DMA((epochs, 2)),
            pltpu.SemaphoreType.DMA((epochs, 2)),
            pltpu.SemaphoreType.DMA((events - 1,)),
            pltpu.SemaphoreType.DMA((events - 1,)),
        ],
        compiler_params=pltpu.CompilerParams(
            collective_id=0, has_side_effects=True, vmem_limit_bytes=40 * 2**20
        ),
        name="adjoint",
    )(adjoint_init, forward_state, p_speed, s_speed, density)


def solution(mesh):
    placed = (
        P("event", None, None, "lon", None),
        P("event", None, None, None, "lon", None),
        P(None, "lon", None),
        P(None, "lon", None),
        P(None, "lon", None),
    )
    return jax.shard_map(
        shards, mesh=mesh, in_specs=placed, out_specs=P(None, "event", "lon", None), check_vma=False
    )
```

```python
import functools

import jax
import jax.numpy as jnp
from jax import lax
from jax.experimental import pallas as pl
from jax.experimental.pallas import tpu as pltpu
from jax.sharding import PartitionSpec as P

VX, VY, VZ, XX, YY, ZZ, XY, XZ, YZ = range(9)
HALO = 4
TILE = 8
PAD = 8
GROUP = 4


def behind_lat(a):
    lane = lax.broadcasted_iota(jnp.int32, a.shape, 1)
    return a - jnp.where(lane == 0, 0.0, pltpu.roll(a, 1, 1))


def ahead_lat(a):
    lane = lax.broadcasted_iota(jnp.int32, a.shape, 1)
    last = a.shape[1] - 1
    return jnp.where(lane == last, 0.0, pltpu.roll(a, last, 1)) - a


def kernel(
    adj_hbm, fwd_hbm, p_hbm, s_hbm, d_hbm, out_ref,
    adj, fwd, p_raw, s_raw, d_raw, w, mat, acc,
    first_out, first_in, next_out, next_in, red_out, red_in,
    local_sem, fwd_sem, halo_send, halo_recv, red_send, red_recv,
):
    levels, own, lat = p_raw.shape
    steps = fwd.shape[0]
    events, ring = lax.axis_size("event"), lax.axis_size("lon")
    me_e, me_l = lax.axis_index("event"), lax.axis_index("lon")
    right, left = lax.rem(me_l + 1, ring), lax.rem(me_l + ring - 1, ring)
    share = levels // events

    local = [
        pltpu.make_async_copy(src, dst, local_sem.at[i])
        for i, (src, dst) in enumerate(
            ((adj_hbm.at[0], adj), (d_hbm, d_raw), (p_hbm, p_raw), (s_hbm, s_raw))
        )
    ]
    for copy in local:
        copy.start()

    def fwd_copy(t):
        return pltpu.make_async_copy(fwd_hbm.at[0, t], fwd.at[t], fwd_sem.at[t])

    barrier = pltpu.get_barrier_semaphore()
    for neighbour in (left, right):
        pl.semaphore_signal(
            barrier, inc=1, device_id=(me_e, neighbour), device_id_type=pl.DeviceIdType.MESH
        )
    for d in range(1, events):
        pl.semaphore_signal(
            barrier, inc=1, device_id=(lax.rem(me_e + d, events), me_l),
            device_id_type=pl.DeviceIdType.MESH,
        )

    zeros = jnp.zeros((w.shape[2], lat), jnp.float32)
    for f in (XZ, YZ, VZ):
        w[f, 0] = zeros
    for f in (ZZ, VX, VY):
        w[f, levels + 1] = zeros

    upper = lax.broadcasted_iota(jnp.int32, (TILE, lat), 0) < HALO

    def pack(get, put):
        def edges(j):
            a, b = get(j, 0), get(j + 1, 0)
            c, d = get(j, own - TILE), get(j + 1, own - TILE)
            return (
                jnp.where(upper, a, pltpu.roll(b, HALO, 0)),
                jnp.where(upper, pltpu.roll(c, HALO, 0), d),
            )

        lo, hi = edges(0), edges(2)
        for side in range(2):
            put(side, jnp.concatenate([lo[side], hi[side]], axis=0).astype(jnp.bfloat16))

    def unpack(from_right, from_left, put):
        r16, l16 = from_right.astype(jnp.float32), from_left.astype(jnp.float32)
        for half in range(2):
            r, l = (v[half * TILE:(half + 1) * TILE] for v in (r16, l16))
            put(2 * half, jnp.where(upper, r, pltpu.roll(l, HALO, 0)))
            put(2 * half + 1, jnp.where(upper, pltpu.roll(r, HALO, 0), l))

    quads = levels // GROUP
    flip = jnp.where(me_e * 2 < events, 1, 0)

    def quad_of(i):
        return i + flip * (quads - 1 - 2 * i)

    def exchange(src, dst, at, i):
        return [
            pltpu.make_async_remote_copy(
                src_ref=src.at[i, side], dst_ref=dst.at[i, side],
                send_sem=halo_send.at[at, i, side], recv_sem=halo_recv.at[at, i, side],
                device_id=(me_e, target), device_id_type=pl.DeviceIdType.MESH,
            )
            for side, target in ((0, left), (1, right))
        ]

    def pack_fields(out, i, q):
        for f in range(9):
            def put(side, value, f=f):
                out[i, side, f] = value

            pack(lambda j, r, f=f: w[f, q * GROUP + j + 1, PAD + r:PAD + r + TILE, :], put)

    for copy in local:
        copy.wait()
    for t in range(steps):
        fwd_copy(t).start()

    def prepare(i, carry):
        q = quad_of(i)
        for j in range(GROUP):
            z = q * GROUP + j
            d, p, s = d_raw[z], p_raw[z], s_raw[z]
            mat[0, z, 0:own, :] = 1.0 / d
            mat[1, z, 0:own, :] = d * (p * p - 2.0 * s * s)
            mat[2, z, 0:own, :] = d * s * s
            for f in range(9):
                rows = adj[f, z].astype(jnp.float32)
                w[f, z + 1, PAD:PAD + own, :] = rows
                if f == XX:
                    w[f, z + 1, PAD + own + TILE:PAD + own + 2 * TILE, :] = rows[:TILE]
        pack_fields(first_out, i, q)
        for f in range(3):
            def put(side, value, f=f):
                first_out[i, side, 9 + f] = value

            pack(lambda j, r, f=f: mat[f, q * GROUP + j, r:r + TILE, :], put)

        @pl.when(i == 0)
        def _():
            pl.semaphore_wait(barrier, events + 1)

        for copy in exchange(first_out, first_in, 0, i):
            copy.start()
        return carry

    lax.fori_loop(0, quads, prepare, 0)

    def receive(epoch, i):
        src, dst = (first_out, first_in) if epoch == 0 else (
            next_out.at[epoch - 1], next_in.at[epoch - 1]
        )
        for copy in exchange(src, dst, epoch, i):
            copy.wait_recv()
        q = quad_of(i)
        for f in range(9):
            def put(j, tile, f=f):
                w[f, q * GROUP + j + 1, PAD + own:PAD + own + TILE, :] = tile
                if f in (XY, XZ):
                    w[f, q * GROUP + j + 1, 0:TILE, :] = tile

            unpack(dst[i, 0, f], dst[i, 1, f], put)
        for f in range(3 if epoch == 0 else 0):
            def put_material(j, tile, f=f):
                mat[f, q * GROUP + j, own:own + TILE, :] = tile

            unpack(dst[i, 0, 9 + f], dst[i, 1, 9 + f], put_material)

    blocks = [(r, 2 * TILE) for r in range(0, own, 2 * TILE)] + [(own, TILE)]

    def velocity_level(z):
        for r, n in blocks:
            def ld(f, off=0, dz=0):
                return w[f, z + 1 + dz, pl.ds(PAD + r + off, n), :]

            buoy = mat[0, z, r:r + n, :]
            xy, xz, yz, zz = ld(XY), ld(XZ), ld(YZ), ld(ZZ)
            fx = (ld(XX, 1) - ld(XX)) + behind_lat(xy) + (xz - ld(XZ, 0, -1))
            fy = (xy - ld(XY, -1)) + ahead_lat(ld(YY)) + (yz - ld(YZ, 0, -1))
            fz = (xz - ld(XZ, -1)) + behind_lat(yz) + (ld(ZZ, 0, 1) - zz)
            for f, force in ((VX, fx), (VY, fy), (VZ, fz)):
                v = ld(f) + buoy * force
                w[f, z + 1, PAD + r:PAD + r + n, :] = v
                if r == 0 and f in (VY, VZ):
                    w[f, z + 1, PAD + own + TILE:PAD + own + 2 * TILE, :] = v[:TILE]
                if r == own and f == VX:
                    w[f, z + 1, 0:TILE, :] = v

    def rates(z, r, n):
        def ld(f, off=0, dz=0):
            return w[f, z + 1 + dz, pl.ds(PAD + r + off, n), :]

        vx, vy, vz = ld(VX), ld(VY), ld(VZ)
        exx = vx - ld(VX, -1)
        eyy = behind_lat(vy)
        ezz = vz - ld(VZ, 0, -1)
        gxy = ahead_lat(vx) + (ld(VY, 1) - vy)
        gxz = (ld(VX, 0, 1) - vx) + (ld(VZ, 1) - vz)
        gyz = (ld(VY, 0, 1) - vy) + ahead_lat(vz)
        return (vx, vy, vz), (exx, eyy, ezz, gxy, gxz, gyz), exx + eyy + ezz

    def terms(t, z, r, n, v, e, tr):
        F = [fwd[t, f, z, r:r + n, :].astype(jnp.float32) for f in range(9)]
        k_lame = tr * (F[3] + F[4] + F[5])
        half_shear = (e[0] * F[3] + e[1] * F[4] + e[2] * F[5]) + (
            e[3] * F[6] + e[4] * F[7] + e[5] * F[8]
        )
        k_dens = v[0] * F[0] + v[1] * F[1] + v[2] * F[2]
        return k_lame, half_shear, k_dens

    def stress_level(t, z):
        for r, n in blocks:
            v, e, tr = rates(z, r, n)
            lame, shear = mat[1, z, r:r + n, :], mat[2, z, r:r + n, :]
            volume, twice = lame * tr, shear + shear
            for i, f in enumerate((XX, YY, ZZ, XY, XZ, YZ)):
                rows = slice(PAD + r, PAD + r + n)
                s = w[f, z + 1, rows, :]
                s = (s + volume) + twice * e[i] if i < 3 else s + shear * e[i]
                w[f, z + 1, rows, :] = s
                if r == 0 and f == XX:
                    w[f, z + 1, PAD + own + TILE:PAD + own + 2 * TILE, :] = s[:TILE]
                if r == own and f in (XY, XZ):
                    w[f, z + 1, 0:TILE, :] = s
            if r < own:
                for i, term in enumerate(terms(t, z, r, n, v, e, tr)):
                    acc[i, z, r:r + n, :] += term

    def clear(z, carry):
        for i in range(3):
            acc[i, z] = jnp.zeros((own, lat), jnp.float32)
        return carry

    lax.fori_loop(0, levels, clear, 0)

    def red_copy(d):
        return pltpu.make_async_remote_copy(
            src_ref=red_out.at[d], dst_ref=red_in.at[d],
            send_sem=red_send.at[d], recv_sem=red_recv.at[d],
            device_id=(lax.rem(me_e + d, events), me_l), device_id_type=pl.DeviceIdType.MESH,
        )

    def velocities(i):
        @pl.when((i >= 0) & (i < quads))
        def _():
            for j in range(GROUP):
                velocity_level(quad_of(i) * GROUP + j)

    def stresses(t, i, then):
        @pl.when((i >= 0) & (i < quads))
        def _():
            @pl.when(i == 0)
            def _():
                fwd_copy(t).wait()

            for j in range(GROUP):
                stress_level(t, quad_of(i) * GROUP + j)
            then(i)

    def totals(t, i):
        @pl.when((i >= 0) & (i < quads))
        def _():
            @pl.when(i == 0)
            def _():
                fwd_copy(t).wait()

            for part in range(GROUP // share):
                owner = quad_of(i) * (GROUP // share) + part
                d = lax.rem(owner - me_e + events, events)
                for j in range(share):
                    z = owner * share + j
                    for r, n in blocks[:-1]:
                        v, e, tr = rates(z, r, n)
                        for k, term in enumerate(terms(t, z, r, n, v, e, tr)):
                            total = acc[k, z, r:r + n, :] + term
                            red_out[d, k, j, r:r + n, :] = total.astype(jnp.bfloat16)

                @pl.when(d != 0)
                def _():
                    red_copy(d).start()

    epochs = -(-steps // HALO)
    for epoch in range(epochs):
        first, count = epoch * HALO, min(HALO, steps - epoch * HALO)
        final = epoch == epochs - 1
        full = count - 1 if final else count

        def send_edges(s, i, epoch=epoch, count=count):
            @pl.when(s == count - 1)
            def _():
                pack_fields(next_out.at[epoch], i, quad_of(i))
                for copy in exchange(next_out.at[epoch], next_in.at[epoch], epoch + 1, i):
                    copy.start()

        def slot(k, carry, epoch=epoch, first=first, full=full, final=final, send=send_edges):
            @pl.when(k < quads)
            def _():
                receive(epoch, k)

            k = k - 1

            def half_steps(s, carry):
                velocities(k - 2 * s)
                stresses(
                    first + s, k - 2 * s - 1, (lambda i: None) if final else lambda i: send(s, i)
                )
                return carry

            low = jnp.maximum(0, (k - quads + 1) // 2)
            high = jnp.minimum(full, (k + 2) // 2)
            lax.fori_loop(low, jnp.maximum(low, high), half_steps, 0)
            if final:
                velocities(k - 2 * full)
                totals(first + full, k - 2 * full - 1)
            return carry

        lax.fori_loop(0, quads + 2 * count, slot, 0)

    def finish(i, carry):
        for epoch in range(epochs):
            src, dst = (first_out, first_in) if epoch == 0 else (
                next_out.at[epoch - 1], next_in.at[epoch - 1]
            )
            for copy in exchange(src, dst, epoch, i):
                copy.wait_send()
        return carry

    lax.fori_loop(0, quads, finish, 0)

    def finish_copies(d, carry):
        red_copy(d).wait()
        return carry

    lax.fori_loop(1, events, finish_copies, 0)

    for j in range(share):
        z = me_e * share + j
        for r, n in blocks[:-1]:
            k_lame, half_shear, k_dens = (
                red_out[0, i, j, r:r + n, :].astype(jnp.float32)
                + sum(red_in[d, i, j, r:r + n, :].astype(jnp.float32) for d in range(1, events))
                for i in range(3)
            )
            k_shear = 2.0 * half_shear
            p, s, d = (x[z, r:r + n, :] for x in (p_raw, s_raw, d_raw))
            lame, shear = d * (p * p - 2.0 * s * s), d * s * s
            out_ref[0, j, r:r + n, :] = 2.0 * d * p * p * k_lame
            out_ref[1, j, r:r + n, :] = 2.0 * d * s * s * (k_shear - 2.0 * k_lame)
            out_ref[2, j, r:r + n, :] = d * k_dens + lame * k_lame + shear * k_shear


def shards(adjoint_init, forward_state, p_speed, s_speed, density):
    levels, own, lat = p_speed.shape
    steps = forward_state.shape[1]
    events = lax.axis_size("event")
    share, quads = levels // events, levels // GROUP
    epochs = -(-steps // HALO)
    f32, bf16 = jnp.float32, jnp.bfloat16
    anywhere = pl.BlockSpec(memory_space=pltpu.HBM)
    return pl.pallas_call(
        kernel,
        out_shape=jax.ShapeDtypeStruct((3, share, own, lat), f32),
        in_specs=[anywhere] * 5,
        out_specs=pl.BlockSpec(memory_space=pltpu.VMEM),
        scratch_shapes=[
            pltpu.VMEM(adjoint_init.shape[1:], bf16),
            pltpu.VMEM(forward_state.shape[1:], bf16),
            pltpu.VMEM(p_speed.shape, f32),
            pltpu.VMEM(p_speed.shape, f32),
            pltpu.VMEM(p_speed.shape, f32),
            pltpu.VMEM((9, levels + 2, PAD + own + 2 * TILE, lat), f32),
            pltpu.VMEM((3, levels, own + TILE, lat), f32),
            pltpu.VMEM((3, levels, own, lat), f32),
            pltpu.VMEM((quads, 2, 12, 2 * TILE, lat), bf16),
            pltpu.VMEM((quads, 2, 12, 2 * TILE, lat), bf16),
            pltpu.VMEM((max(epochs - 1, 1), quads, 2, 9, 2 * TILE, lat), bf16),
            pltpu.VMEM((max(epochs - 1, 1), quads, 2, 9, 2 * TILE, lat), bf16),
            pltpu.VMEM((events, 3, share, own, lat), bf16),
            pltpu.VMEM((events, 3, share, own, lat), bf16),
            pltpu.SemaphoreType.DMA((4,)),
            pltpu.SemaphoreType.DMA((steps,)),
            pltpu.SemaphoreType.DMA((epochs, quads, 2)),
            pltpu.SemaphoreType.DMA((epochs, quads, 2)),
            pltpu.SemaphoreType.DMA((events,)),
            pltpu.SemaphoreType.DMA((events,)),
        ],
        compiler_params=pltpu.CompilerParams(
            collective_id=0, has_side_effects=True, vmem_limit_bytes=60 * 2**20
        ),
        name="adjoint",
    )(adjoint_init, forward_state, p_speed, s_speed, density)


def solution(mesh):
    placed = (
        P("event", None, None, "lon", None),
        P("event", None, None, None, "lon", None),
        P(None, "lon", None),
        P(None, "lon", None),
        P(None, "lon", None),
    )
    return jax.shard_map(
        shards, mesh=mesh, in_specs=placed, out_specs=P(None, "event", "lon", None), check_vma=False
    )
```

```python
import functools

import jax
import jax.numpy as jnp
from jax import lax
from jax.experimental import pallas as pl
from jax.experimental.pallas import tpu as pltpu
from jax.sharding import PartitionSpec as P

VX, VY, VZ, XX, YY, ZZ, XY, XZ, YZ = range(9)
HALO = 4
TILE = 8
PAD = 8
GROUP = 4


def behind_lat(a):
    lane = lax.broadcasted_iota(jnp.int32, a.shape, 1)
    return a - jnp.where(lane == 0, 0.0, pltpu.roll(a, 1, 1))


def ahead_lat(a):
    lane = lax.broadcasted_iota(jnp.int32, a.shape, 1)
    last = a.shape[1] - 1
    return jnp.where(lane == last, 0.0, pltpu.roll(a, last, 1)) - a


def kernel(
    adj_hbm, fwd_hbm, p_hbm, s_hbm, d_hbm, out_ref,
    adj, fwd, p_raw, s_raw, d_raw, w, mat, acc,
    first_out, first_in, next_out, next_in, red_out, red_in,
    local_sem, fwd_sem, halo_send, halo_recv, red_send, red_recv,
):
    levels, own, lat = p_raw.shape
    steps = fwd.shape[0]
    events, ring = lax.axis_size("event"), lax.axis_size("lon")
    me_e, me_l = lax.axis_index("event"), lax.axis_index("lon")
    right, left = lax.rem(me_l + 1, ring), lax.rem(me_l + ring - 1, ring)
    share = levels // events

    quads = levels // GROUP
    flip = jnp.where(me_e * 2 < events, 1, 0)

    def quad_of(i):
        return i + flip * (quads - 1 - 2 * i)

    def local_copies(i):
        rows = pl.ds(quad_of(i) * GROUP, GROUP)
        pairs = (
            (adj_hbm.at[0, :, rows], adj.at[:, rows]),
            (d_hbm.at[rows], d_raw.at[rows]),
            (p_hbm.at[rows], p_raw.at[rows]),
            (s_hbm.at[rows], s_raw.at[rows]),
        )
        return [
            pltpu.make_async_copy(src, dst, local_sem.at[i, k])
            for k, (src, dst) in enumerate(pairs)
        ]

    for i in range(quads):
        for copy in local_copies(i):
            copy.start()

    def fwd_copy(t):
        return pltpu.make_async_copy(fwd_hbm.at[0, t], fwd.at[t], fwd_sem.at[t])

    barrier = pltpu.get_barrier_semaphore()
    for neighbour in (left, right):
        pl.semaphore_signal(
            barrier, inc=1, device_id=(me_e, neighbour), device_id_type=pl.DeviceIdType.MESH
        )
    for d in range(1, events):
        pl.semaphore_signal(
            barrier, inc=1, device_id=(lax.rem(me_e + d, events), me_l),
            device_id_type=pl.DeviceIdType.MESH,
        )

    zeros = jnp.zeros((w.shape[2], lat), jnp.float32)
    for f in (XZ, YZ, VZ):
        w[f, 0] = zeros
    for f in (ZZ, VX, VY):
        w[f, levels + 1] = zeros

    upper = lax.broadcasted_iota(jnp.int32, (TILE, lat), 0) < HALO

    def pack(get, put):
        def edges(j):
            a, b = get(j, 0), get(j + 1, 0)
            c, d = get(j, own - TILE), get(j + 1, own - TILE)
            return (
                jnp.where(upper, a, pltpu.roll(b, HALO, 0)),
                jnp.where(upper, pltpu.roll(c, HALO, 0), d),
            )

        lo, hi = edges(0), edges(2)
        for side in range(2):
            put(side, jnp.concatenate([lo[side], hi[side]], axis=0).astype(jnp.bfloat16))

    def unpack(from_right, from_left, put):
        r16, l16 = from_right.astype(jnp.float32), from_left.astype(jnp.float32)
        for half in range(2):
            r, l = (v[half * TILE:(half + 1) * TILE] for v in (r16, l16))
            put(2 * half, jnp.where(upper, r, pltpu.roll(l, HALO, 0)))
            put(2 * half + 1, jnp.where(upper, pltpu.roll(r, HALO, 0), l))

    def exchange(src, dst, at, i):
        return [
            pltpu.make_async_remote_copy(
                src_ref=src.at[i, side], dst_ref=dst.at[i, side],
                send_sem=halo_send.at[at, i, side], recv_sem=halo_recv.at[at, i, side],
                device_id=(me_e, target), device_id_type=pl.DeviceIdType.MESH,
            )
            for side, target in ((0, left), (1, right))
        ]

    def pack_fields(out, i, q):
        for f in range(9):
            def put(side, value, f=f):
                out[i, side, f] = value

            pack(lambda j, r, f=f: w[f, q * GROUP + j + 1, PAD + r:PAD + r + TILE, :], put)

    for t in range(steps):
        fwd_copy(t).start()

    def prepare(i, carry):
        q = quad_of(i)
        for copy in local_copies(i):
            copy.wait()
        for j in range(GROUP):
            z = q * GROUP + j
            d, p, s = d_raw[z], p_raw[z], s_raw[z]
            mat[0, z, 0:own, :] = 1.0 / d
            mat[1, z, 0:own, :] = d * (p * p - 2.0 * s * s)
            mat[2, z, 0:own, :] = d * s * s
            for f in range(9):
                rows = adj[f, z].astype(jnp.float32)
                w[f, z + 1, PAD:PAD + own, :] = rows
                if f == XX:
                    w[f, z + 1, PAD + own + TILE:PAD + own + 2 * TILE, :] = rows[:TILE]
        pack_fields(first_out, i, q)
        for f in range(3):
            def put(side, value, f=f):
                first_out[i, side, 9 + f] = value

            pack(lambda j, r, f=f: mat[f, q * GROUP + j, r:r + TILE, :], put)

        @pl.when(i == 0)
        def _():
            pl.semaphore_wait(barrier, events + 1)

        for copy in exchange(first_out, first_in, 0, i):
            copy.start()
        return carry

    lax.fori_loop(0, quads, prepare, 0)

    def receive(epoch, i):
        src, dst = (first_out, first_in) if epoch == 0 else (
            next_out.at[epoch - 1], next_in.at[epoch - 1]
        )
        for copy in exchange(src, dst, epoch, i):
            copy.wait_recv()
        q = quad_of(i)
        for f in range(9):
            def put(j, tile, f=f):
                w[f, q * GROUP + j + 1, PAD + own:PAD + own + TILE, :] = tile
                if f in (XY, XZ):
                    w[f, q * GROUP + j + 1, 0:TILE, :] = tile

            unpack(dst[i, 0, f], dst[i, 1, f], put)
        for f in range(3 if epoch == 0 else 0):
            def put_material(j, tile, f=f):
                mat[f, q * GROUP + j, own:own + TILE, :] = tile

            unpack(dst[i, 0, 9 + f], dst[i, 1, 9 + f], put_material)

    blocks = [(r, 2 * TILE) for r in range(0, own, 2 * TILE)] + [(own, TILE)]

    def velocity_levels(q):
        for r, n in blocks:
            below = None
            for j in range(GROUP):
                z = q * GROUP + j

                def ld(f, off=0, dz=0):
                    return w[f, z + 1 + dz, pl.ds(PAD + r + off, n), :]

                if j == 0:
                    below = (ld(XZ, 0, -1), ld(YZ, 0, -1))
                    zz = ld(ZZ)
                buoy = mat[0, z, r:r + n, :]
                xy, xz, yz, above = ld(XY), ld(XZ), ld(YZ), ld(ZZ, 0, 1)
                fx = (ld(XX, 1) - ld(XX)) + behind_lat(xy) + (xz - below[0])
                fy = (xy - ld(XY, -1)) + ahead_lat(ld(YY)) + (yz - below[1])
                fz = (xz - ld(XZ, -1)) + behind_lat(yz) + (above - zz)
                below, zz = (xz, yz), above
                for f, force in ((VX, fx), (VY, fy), (VZ, fz)):
                    v = ld(f) + buoy * force
                    w[f, z + 1, PAD + r:PAD + r + n, :] = v
                    if r == 0 and f in (VY, VZ):
                        w[f, z + 1, PAD + own + TILE:PAD + own + 2 * TILE, :] = v[:TILE]
                    if r == own and f == VX:
                        w[f, z + 1, 0:TILE, :] = v

    def rates(z, r, n, held):
        def ld(f, off=0, dz=0):
            return w[f, z + 1 + dz, pl.ds(PAD + r + off, n), :]

        vx, vy, behind = held or (ld(VX), ld(VY), ld(VZ, 0, -1))
        vz, above_x, above_y = ld(VZ), ld(VX, 0, 1), ld(VY, 0, 1)
        exx = vx - ld(VX, -1)
        eyy = behind_lat(vy)
        ezz = vz - behind
        gxy = ahead_lat(vx) + (ld(VY, 1) - vy)
        gxz = (above_x - vx) + (ld(VZ, 1) - vz)
        gyz = (above_y - vy) + ahead_lat(vz)
        held = (above_x, above_y, vz)
        return (vx, vy, vz), (exx, eyy, ezz, gxy, gxz, gyz), exx + eyy + ezz, held

    def terms(t, z, r, n, v, e, tr):
        F = [fwd[t, f, z, r:r + n, :].astype(jnp.float32) for f in range(9)]
        k_lame = tr * (F[3] + F[4] + F[5])
        half_shear = (e[0] * F[3] + e[1] * F[4] + e[2] * F[5]) + (
            e[3] * F[6] + e[4] * F[7] + e[5] * F[8]
        )
        k_dens = v[0] * F[0] + v[1] * F[1] + v[2] * F[2]
        return k_lame, half_shear, k_dens

    def stress_levels(t, q):
        for r, n in blocks:
            held = None
            for j in range(GROUP):
                z = q * GROUP + j
                v, e, tr, held = rates(z, r, n, held)
                lame, shear = mat[1, z, r:r + n, :], mat[2, z, r:r + n, :]
                volume, twice = lame * tr, shear + shear
                for i, f in enumerate((XX, YY, ZZ, XY, XZ, YZ)):
                    rows = slice(PAD + r, PAD + r + n)
                    s = w[f, z + 1, rows, :]
                    s = (s + volume) + twice * e[i] if i < 3 else s + shear * e[i]
                    w[f, z + 1, rows, :] = s
                    if r == 0 and f == XX:
                        w[f, z + 1, PAD + own + TILE:PAD + own + 2 * TILE, :] = s[:TILE]
                    if r == own and f in (XY, XZ):
                        w[f, z + 1, 0:TILE, :] = s
                if r < own:
                    for i, term in enumerate(terms(t, z, r, n, v, e, tr)):
                        acc[i, z, r:r + n, :] += term

    def clear(z, carry):
        for i in range(3):
            acc[i, z] = jnp.zeros((own, lat), jnp.float32)
        return carry

    lax.fori_loop(0, levels, clear, 0)

    def red_copy(d):
        return pltpu.make_async_remote_copy(
            src_ref=red_out.at[d], dst_ref=red_in.at[d],
            send_sem=red_send.at[d], recv_sem=red_recv.at[d],
            device_id=(lax.rem(me_e + d, events), me_l), device_id_type=pl.DeviceIdType.MESH,
        )

    def velocities(i):
        @pl.when((i >= 0) & (i < quads))
        def _():
            velocity_levels(quad_of(i))

    def stresses(t, i, then):
        @pl.when((i >= 0) & (i < quads))
        def _():
            @pl.when(i == 0)
            def _():
                fwd_copy(t).wait()

            stress_levels(t, quad_of(i))
            then(i)

    def totals(t, i):
        @pl.when((i >= 0) & (i < quads))
        def _():
            @pl.when(i == 0)
            def _():
                fwd_copy(t).wait()

            for part in range(GROUP // share):
                owner = quad_of(i) * (GROUP // share) + part
                d = lax.rem(owner - me_e + events, events)
                for r, n in blocks[:-1]:
                    held = None
                    for j in range(share):
                        z = owner * share + j
                        v, e, tr, held = rates(z, r, n, held)
                        for k, term in enumerate(terms(t, z, r, n, v, e, tr)):
                            total = acc[k, z, r:r + n, :] + term
                            red_out[d, k, j, r:r + n, :] = total.astype(jnp.bfloat16)

                @pl.when(d != 0)
                def _():
                    red_copy(d).start()

    epochs = -(-steps // HALO)
    for epoch in range(epochs):
        first, count = epoch * HALO, min(HALO, steps - epoch * HALO)
        final = epoch == epochs - 1
        full = count - 1 if final else count

        def send_edges(s, i, epoch=epoch, count=count):
            @pl.when(s == count - 1)
            def _():
                pack_fields(next_out.at[epoch], i, quad_of(i))
                for copy in exchange(next_out.at[epoch], next_in.at[epoch], epoch + 1, i):
                    copy.start()

        def slot(k, carry, epoch=epoch, first=first, full=full, final=final, send=send_edges):
            @pl.when(k < quads)
            def _():
                receive(epoch, k)

            k = k - 1

            def half_steps(s, carry):
                velocities(k - 2 * s)
                stresses(
                    first + s, k - 2 * s - 1, (lambda i: None) if final else lambda i: send(s, i)
                )
                return carry

            low = jnp.maximum(0, (k - quads + 1) // 2)
            high = jnp.minimum(full, (k + 2) // 2)
            lax.fori_loop(low, jnp.maximum(low, high), half_steps, 0)
            if final:
                velocities(k - 2 * full)
                totals(first + full, k - 2 * full - 1)
            return carry

        lax.fori_loop(0, quads + 2 * count, slot, 0)

    def finish(i, carry):
        for epoch in range(epochs):
            src, dst = (first_out, first_in) if epoch == 0 else (
                next_out.at[epoch - 1], next_in.at[epoch - 1]
            )
            for copy in exchange(src, dst, epoch, i):
                copy.wait_send()
        return carry

    lax.fori_loop(0, quads, finish, 0)

    def finish_copies(d, carry):
        red_copy(d).wait()
        return carry

    lax.fori_loop(1, events, finish_copies, 0)

    for j in range(share):
        z = me_e * share + j
        for r, n in blocks[:-1]:
            k_lame, half_shear, k_dens = (
                red_out[0, i, j, r:r + n, :].astype(jnp.float32)
                + sum(red_in[d, i, j, r:r + n, :].astype(jnp.float32) for d in range(1, events))
                for i in range(3)
            )
            k_shear = 2.0 * half_shear
            p, s, d = (x[z, r:r + n, :] for x in (p_raw, s_raw, d_raw))
            lame, shear = d * (p * p - 2.0 * s * s), d * s * s
            out_ref[0, j, r:r + n, :] = 2.0 * d * p * p * k_lame
            out_ref[1, j, r:r + n, :] = 2.0 * d * s * s * (k_shear - 2.0 * k_lame)
            out_ref[2, j, r:r + n, :] = d * k_dens + lame * k_lame + shear * k_shear


def shards(adjoint_init, forward_state, p_speed, s_speed, density):
    levels, own, lat = p_speed.shape
    steps = forward_state.shape[1]
    events = lax.axis_size("event")
    share, quads = levels // events, levels // GROUP
    epochs = -(-steps // HALO)
    f32, bf16 = jnp.float32, jnp.bfloat16
    anywhere = pl.BlockSpec(memory_space=pltpu.HBM)
    return pl.pallas_call(
        kernel,
        out_shape=jax.ShapeDtypeStruct((3, share, own, lat), f32),
        in_specs=[anywhere] * 5,
        out_specs=pl.BlockSpec(memory_space=pltpu.VMEM),
        scratch_shapes=[
            pltpu.VMEM(adjoint_init.shape[1:], bf16),
            pltpu.VMEM(forward_state.shape[1:], bf16),
            pltpu.VMEM(p_speed.shape, f32),
            pltpu.VMEM(p_speed.shape, f32),
            pltpu.VMEM(p_speed.shape, f32),
            pltpu.VMEM((9, levels + 2, PAD + own + 2 * TILE, lat), f32),
            pltpu.VMEM((3, levels, own + TILE, lat), f32),
            pltpu.VMEM((3, levels, own, lat), f32),
            pltpu.VMEM((quads, 2, 12, 2 * TILE, lat), bf16),
            pltpu.VMEM((quads, 2, 12, 2 * TILE, lat), bf16),
            pltpu.VMEM((max(epochs - 1, 1), quads, 2, 9, 2 * TILE, lat), bf16),
            pltpu.VMEM((max(epochs - 1, 1), quads, 2, 9, 2 * TILE, lat), bf16),
            pltpu.VMEM((events, 3, share, own, lat), bf16),
            pltpu.VMEM((events, 3, share, own, lat), bf16),
            pltpu.SemaphoreType.DMA((quads, 4)),
            pltpu.SemaphoreType.DMA((steps,)),
            pltpu.SemaphoreType.DMA((epochs, quads, 2)),
            pltpu.SemaphoreType.DMA((epochs, quads, 2)),
            pltpu.SemaphoreType.DMA((events,)),
            pltpu.SemaphoreType.DMA((events,)),
        ],
        compiler_params=pltpu.CompilerParams(
            collective_id=0, has_side_effects=True, vmem_limit_bytes=60 * 2**20
        ),
        name="adjoint",
    )(adjoint_init, forward_state, p_speed, s_speed, density)


def solution(mesh):
    placed = (
        P("event", None, None, "lon", None),
        P("event", None, None, None, "lon", None),
        P(None, "lon", None),
        P(None, "lon", None),
        P(None, "lon", None),
    )
    return jax.shard_map(
        shards, mesh=mesh, in_specs=placed, out_specs=P(None, "event", "lon", None), check_vma=False
    )
```
